32 devices in a mesh: row: 4 (over z), col: 8 (over y, x, core).
Axes of the slice: x: 2, y: 2, z: 4, core: 2. Of those that a mesh axis runs over, the one named last changes fastest.
Arguments:
- operator: float32 [4096, 4096], P('row', 'col'), may hold values from -0.09375 to 0.09375
- vectors: float32 [4096, 256], P('row', 'col'), may hold values from -6 to 6
- owner_map: int32 [2816, 1], P(('row', 'col')), may hold values from 0 to 7; in each aligned block of 88 rows (0 to 87, 88 to 175, ...) at most 32 rows name the same one
- coupling: float32 [4, 256, 256], P('row', 'col'), may hold values from -0.375 to 0.375
- ancestors: int32 [4, 8, 512], P('row', 'col'), may hold values from 0 to 511, as said below
- leaf_modes: float32 [4, 8, 2048, 256], P('row', 'col'), may hold values from -0.375 to 0.375
- constraint_modes: float32 [4, 8, 2048, 512], P('row', 'col'), may hold values from -0.25 to 0.25
Outputs:
- separators: float32 [4, 256, 256], P('row', 'col')
- interiors: float32 [4, 8, 2048, 256], P('row', 'col')
The draws below stay inside these ranges and needn't reach their ends.
Inputs may be any that keep to these rules, and one draw needn't show every extreme that they name: `owner_map`: in each aligned block of 88 rows no leaf is named more than 32 times, a bound that some block reaches. `ancestors`: the 512 indices of one leaf are distinct.
All inputs are finite; a program needn't handle non-finite values.
Results may differ from the reference program's by a relative error of at most 0.00007.
Values sent between devices are 32-bit elements; how exact they have to be, the bound alone decides.
No kernel may reach another device: no remote copies, remote signals or barrier semaphores. Data moves between devices by JAX's collectives and lax.ppermute only.
A program may use at most 64 MiB of HBM per device.

```python
import math
import jax
import jax.numpy as jnp
import numpy as np
from jax import lax

NV = 256
MODES = 256
INTER = 2048
ANC = 512
MODE_DEV = 88
SEP_DEV = 32
ROWS_DEV = 128
SUBS = 4
FANOUT = 8
M = 4096
MOST = 32
OWNED = 2816
TOPU = 256
SEPU = 256


def draw_ancestors(key, part):
    candidate_total = TOPU + SEPU
    leaf_keys = jax.random.split(key, SUBS * FANOUT)
    selected = jax.vmap(lambda leaf_key: jax.random.permutation(leaf_key, candidate_total)[:ANC])(leaf_keys)
    interior_pick = jax.random.permutation(jax.random.fold_in(key, 7), candidate_total - 2)[:ANC - 2] + 1
    leading = jnp.concatenate([jnp.array([0, candidate_total - 1], jnp.int32), interior_pick.astype(jnp.int32)])
    selected = selected.astype(jnp.int32).at[0].set(leading)
    return selected.reshape(SUBS, FANOUT, ANC)


def shard_levels(stream_key, shape, pieces, low, top_value):
    def one(position, blocks):
        steps = jax.random.uniform(jax.random.fold_in(jax.random.fold_in(stream_key, 6), position), (blocks,), jnp.float32, low / len(pieces), top_value / len(pieces))
        return jnp.repeat(jnp.exp(steps), shape[position] // blocks).reshape((-1,) + (1,) * (len(shape) - position - 1))

    loudness = one(*pieces[0])
    for cut in pieces[1:]:
        loudness = loudness * one(*cut)
    return loudness


def assign_block(rng, own, number, rows, count, top, reach, slope):
    order = jax.random.permutation(rng, count)
    crowded, usual = portions_of(count, rows * top, reach, slope, True), portions_of(count, rows * top, reach, slope, False)
    places = jnp.arange(count)

    def named(sizes, turn):
        used = int((sizes > 0).sum())
        fixed = max(1, used // 4)
        shifted = fixed + (places - fixed + turn * (used - fixed)) % max(1, count - fixed)
        return jnp.zeros((count,), jnp.int32).at[order[jnp.where(places < fixed, places, shifted)]].set(jnp.asarray(sizes, jnp.int32))

    sizes = jnp.where(number % 4 == 0, named(crowded, number // 4), named(usual, number - number // 4 - 1))
    mixed = jax.random.permutation(jax.random.fold_in(own, 3), count)
    donor, receiver = mixed[0:count // 2 * 2:2], mixed[1:count // 2 * 2:2]
    margin = jnp.minimum(sizes[donor] - 1, reach - sizes[receiver]) // 2
    margin = jnp.where((donor == order[0]) | (receiver == order[0]) | (sizes[receiver] == 0), 0, jnp.maximum(margin, 0))
    shifted = jax.random.randint(jax.random.fold_in(own, 4), (count // 2,), 0, 1 << 20) % (margin + 1)
    sizes = sizes.at[donor].add(-shifted).at[receiver].add(shifted)
    items = jnp.searchsorted(jnp.cumsum(sizes), jnp.arange(rows * top), side="right").astype(jnp.int32)
    table = items.reshape(top, rows).T
    table = table[jax.random.permutation(jax.random.fold_in(own, 1), rows)]
    turn = jax.random.randint(jax.random.fold_in(own, 2), (rows, 1), 0, top)
    return jnp.take_along_axis(table, (jnp.arange(top)[None, :] + turn) % top, axis=1)


def portions_of(amount, total, most, skew, full):
    loads = [(1 << 20) // math.isqrt(grade ** skew) + 1 for grade in range(1, amount + 1)]
    largest = most if full else min(most, max(-(-total // amount), total * loads[0] // sum(loads)))
    least = 1 if total - largest >= amount - 1 else 0
    given, spare = [largest] + [least] * (amount - 1), total - largest - least * (amount - 1)
    while spare > 0:
        free = [i for i in range(1, amount) if given[i] < largest] or [i for i in range(1, amount) if given[i] < most]
        mass, budget = sum([loads[i] for i in free]), spare
        for i in free:
            extra = min(most - given[i], max(1, budget * loads[i] // mass), spare)
            given[i] = given[i] + extra
            spare = spare - extra
    return np.array(given)


def bell_draw(rng, shape, scale, limit, cuts=(), kind=jnp.bfloat16):
    values = jax.random.normal(rng, shape, jnp.float32) * scale
    if len(cuts) > 0:
        values = shard_levels(rng, shape, cuts, -0.22, 0.18) * values
    return jnp.clip(values, min=-limit, max=limit).astype(kind)


def setup_inputs(seed: int = 0) -> dict:
    key_of = jax.random.split(jax.random.key(seed), 8)
    operator = bell_draw(key_of[0], (M, M), M ** -0.5, 0.09375, ((0, 4), (1, 8)), jnp.float32)
    vectors = bell_draw(key_of[1], (M, NV), 1.0, 6.0, ((0, 4), (1, 8)), jnp.float32)
    owner_map_keys = jax.random.split(jax.random.fold_in(key_of[2], 1), OWNED // MODE_DEV)
    owner_map_turns = jax.random.permutation(jax.random.fold_in(key_of[2], 3), OWNED // MODE_DEV)
    owner_map = jax.vmap(lambda own, number: assign_block(jax.random.fold_in(key_of[2], 2), own, number, MODE_DEV, FANOUT, 1, MOST, 2))(owner_map_keys, owner_map_turns).reshape((OWNED, 1))
    coupling = bell_draw(key_of[3], (SUBS, SEPU, TOPU), TOPU ** -0.5, 0.375, ((0, 4), (1, 8)), jnp.float32)
    ancestors = draw_ancestors(jax.random.fold_in(key_of[7], 71), 0)
    leaf_modes = bell_draw(key_of[5], (SUBS, FANOUT, INTER, MODES), MODES ** -0.5, 0.375, ((0, 4), (1, 8)), jnp.float32)
    constraint_modes = bell_draw(key_of[6], (SUBS, FANOUT, INTER, ANC), ANC ** -0.5, 0.25, ((0, 4), (1, 8)), jnp.float32)
    return {"operator": operator, "vectors": vectors, "owner_map": owner_map, "coupling": coupling, "ancestors": ancestors, "leaf_modes": leaf_modes, "constraint_modes": constraint_modes}


highest = lax.Precision.HIGHEST


def slot_ranks(owned_rows, fanout):
    onehot = (owned_rows[..., None] == jnp.arange(fanout, dtype=jnp.int32)).astype(jnp.int32)
    running = jnp.cumsum(onehot, axis=-2)
    return jnp.sum(running * onehot, axis=-1) - 1


def pick_rows(candidate_rows, index_rows):
    return jnp.take(candidate_rows, index_rows, axis=0)


def reference(operator, vectors, owner_map, coupling, ancestors, leaf_modes, constraint_modes):
    adjoint = jnp.dot(operator.T, vectors, precision=highest, preferred_element_type=jnp.float32)
    forward = jnp.dot(operator, adjoint, precision=highest, preferred_element_type=jnp.float32)
    blocks = forward.reshape(SUBS * FANOUT, ROWS_DEV, NV)
    mode_rows = blocks[:, :MODE_DEV].reshape(SUBS, FANOUT, MODE_DEV, NV)
    separator_raw = blocks[:, MODE_DEV:MODE_DEV + SEP_DEV].reshape(SUBS, SEPU, NV)
    top_rows = blocks[:, MODE_DEV + SEP_DEV:].reshape(TOPU, NV)
    owned_rows = owner_map[:, 0].reshape(SUBS, FANOUT, MODE_DEV)
    target = owned_rows * MOST + slot_ranks(owned_rows, FANOUT)
    sub_index = jnp.arange(SUBS, dtype=jnp.int32)[:, None, None]
    source_index = jnp.arange(FANOUT, dtype=jnp.int32)[None, :, None]
    buffer = jnp.zeros((SUBS, FANOUT, FANOUT * MOST, NV), jnp.float32)
    buffer = buffer.at[sub_index, source_index, target].set(mode_rows)
    coords = buffer.reshape(SUBS, FANOUT, FANOUT, MOST, NV).transpose(0, 2, 1, 3, 4).reshape(SUBS, FANOUT, MODES, NV)
    separators = separator_raw + jnp.einsum("rst,tv->rsv", coupling, top_rows, precision=highest)
    candidates = jnp.concatenate([jnp.broadcast_to(top_rows, (SUBS, TOPU, NV)), separators], axis=1)
    gathered = jax.vmap(pick_rows)(candidates, ancestors)
    interiors = jnp.einsum("rcim,rcmv->rciv", leaf_modes, coords, precision=highest)
    interiors = interiors + jnp.einsum("rcia,rcav->rciv", constraint_modes, gathered, precision=highest)
    return separators, interiors
```

```python
import jax
import jax.numpy as jnp
from jax import lax
from jax.sharding import PartitionSpec as P

HIGH = lax.Precision.HIGH


def product(a, b, da, db):
    return lax.dot_general(
        a,
        b,
        (((da,), (db,)), ((), ())),
        precision=HIGH,
        preferred_element_type=jnp.float32,
    )


def swap(v, axis, mask):
    n = lax.axis_size(axis)
    return lax.ppermute(v, axis, [(i, i ^ mask) for i in range(n)])


def gather_xor(v, axis, masks):
    blocks = v[None]
    order = [0]
    for mask in masks:
        blocks = jnp.concatenate([blocks, swap(blocks, axis, mask)], axis=0)
        order = order + [o ^ mask for o in order]
    return blocks, order


def arrange(blocks, order, me):
    position = jnp.asarray([order.index(o) for o in range(len(order))], jnp.int32)
    return jnp.stack(
        [
            lax.dynamic_index_in_dim(blocks, position[jnp.int32(i) ^ me], 0, keepdims=False)
            for i in range(len(order))
        ]
    )


def reduce_xor(parts, axis, masks):
    n = len(masks)
    for step in range(n):
        moved = [swap(p, axis, masks[(i + step) % n]) for i, p in enumerate(parts)]
        parts = [p + q for p, q in zip(parts, moved)]
    return parts


def slot_ranks(owned_rows, fanout):
    onehot = (owned_rows[..., None] == jnp.arange(fanout, dtype=jnp.int32)).astype(jnp.int32)
    running = jnp.cumsum(onehot, axis=-2)
    return jnp.sum(running * onehot, axis=-1) - 1


def on_device(operator, vectors, owner_map, coupling, ancestors, leaf_modes, constraint_modes):
    rows = lax.axis_size("row")
    fanout = lax.axis_size("col")
    r = lax.axis_index("row")
    c = lax.axis_index("col")
    mode_local = owner_map.shape[0]
    separator_local = coupling.shape[1]
    top_count = coupling.shape[2]
    mode_count = leaf_modes.shape[3]
    ancestor_count = constraint_modes.shape[3]
    slot_count = mode_count // fanout
    row_count = operator.shape[0]
    block = row_count // fanout
    top_local = block - mode_local - separator_local
    row_masks = [(2 << b) - 1 for b in range(rows.bit_length() - 1)]
    col_masks = [1 << b for b in range(1, fanout.bit_length() - 1)]
    half = fanout // 2

    partner = swap(operator, "col", 1)
    width = coupling.shape[2]
    tags = owner_map[:, 0].astype(jnp.float32)
    tag_rows = -(-mode_local // width)
    tags = jnp.pad(tags, (0, tag_rows * width - mode_local)).reshape(tag_rows, width)
    small = jnp.concatenate([coupling[0], jnp.pad(tags, ((0, -tag_rows % 8), (0, 0)))], axis=0)
    small, small_order = gather_xor(small, "col", [1] + col_masks)
    small = arrange(small, small_order, c)
    coupling_all = small[:, :separator_local].reshape(fanout * separator_local, width)
    owners = small[:, separator_local : separator_local + tag_rows].reshape(fanout, -1)[:, :mode_local]
    owners = owners.astype(jnp.int32)

    blocks, order = gather_xor(vectors.T, "col", col_masks)
    xt = arrange(blocks, [o >> 1 for o in order], c // 2).reshape(-1, operator.shape[0])
    part_a = product(xt, operator, 1, 0)
    part_b = product(xt, partner, 1, 0)
    adj_a, adj_b = reduce_xor([part_a, part_b], "row", row_masks)

    def forward(k, p):
        return product(adj_a, k, 1, 1) + product(adj_b, p, 1, 1)

    def tops(k):
        return k.reshape(fanout, block, -1)[:, block - top_local :].reshape(fanout * top_local, -1)

    top_part, top_order = gather_xor(forward(tops(operator), tops(partner)), "row", row_masks)
    nv_half = xt.shape[0]
    top_part = top_part.transpose(1, 0, 2).reshape(nv_half, top_count)
    cut = row_count // 2
    f0 = forward(operator[:cut], partner[:cut])
    f1 = forward(operator[cut:], partner[cut:])
    f1 = jnp.concatenate([f1, top_part], axis=1)
    f0, f1 = reduce_xor([f0, f1], "col", col_masks)
    own = jnp.concatenate([f0, f1], axis=1)
    other = swap(own, "col", 1)
    even = jnp.where(c % 2 == 0, own, other)
    odd = jnp.where(c % 2 == 0, other, own)
    width = own.shape[1]
    full = jnp.stack([even.reshape(half, -1, width), odd.reshape(half, -1, width)], axis=1).reshape(-1, width)

    ranks = slot_ranks(owners, fanout)
    slot = jnp.where(owners == c, jnp.arange(fanout, dtype=jnp.int32)[:, None] * slot_count + ranks, -1)
    slot = jnp.concatenate([slot, jnp.full((fanout, block - mode_local), -1, jnp.int32)], axis=1).reshape(-1)
    pick_modes = (slot[:, None] == jnp.arange(mode_count, dtype=jnp.int32)).astype(jnp.float32)
    top_plane = fanout * top_local
    top_inverse = jnp.asarray([top_order.index(o) for o in range(rows)], jnp.int32)
    top_place = top_inverse[jnp.arange(rows, dtype=jnp.int32) ^ r]
    anc = ancestors[0, 0]
    top_full = full[:, row_count:].reshape(-1, rows, top_plane)
    top_full = jnp.take(top_full, top_place, axis=1).reshape(-1, top_count)
    raw = full[:, :row_count].reshape(-1, fanout, block)[:, :, mode_local : mode_local + separator_local]
    raw = raw.reshape(-1, fanout * separator_local)
    sep = raw + product(top_full, coupling_all, 1, 1)
    candidates = jnp.concatenate([top_full, sep], axis=1)
    pick_anc = (jnp.arange(candidates.shape[1], dtype=jnp.int32)[:, None] == anc).astype(jnp.float32)
    highest = lax.Precision.HIGHEST
    coords = jnp.dot(full[:, :row_count], pick_modes, precision=highest)
    gathered = jnp.dot(candidates, pick_anc, precision=highest)
    interiors = product(leaf_modes[0, 0], coords, 1, 1) + product(constraint_modes[0, 0], gathered, 1, 1)
    sep_own = lax.dynamic_slice_in_dim(sep, c * separator_local, separator_local, axis=1).T
    return (sep_own[None], interiors[None, None])


def solution(mesh):
    in_specs = (
        P("row", "col"),
        P("row", "col"),
        P(("row", "col"), None),
        P("row", "col", None),
        P("row", "col", None),
        P("row", "col", None, None),
        P("row", "col", None, None),
    )
    out_specs = (P("row", "col", None), P("row", "col", None, None))
    return jax.shard_map(
        on_device, mesh=mesh, in_specs=in_specs, out_specs=out_specs, check_vma=False
    )
```

```python
import jax
import jax.numpy as jnp
from jax import lax
from jax.experimental import pallas as pl
from jax.experimental.pallas import tpu as pltpu
from jax.sharding import PartitionSpec as P


F32, BF16 = jnp.float32, jnp.bfloat16
NN = (((1,), (0,)), ((), ()))
NT = (((1,), (1,)), ((), ()))


def swap(v, axis, mask):
    n = lax.axis_size(axis)
    return lax.ppermute(v, axis, [(i, i ^ mask) for i in range(n)])


def call(body, out, *args, scratch=(), flops=0):
    size = sum(a.size * a.dtype.itemsize for a in args) + sum(
        o.size * o.dtype.itemsize for o in out
    )
    specs = [pl.BlockSpec(memory_space=pltpu.VMEM)] * len(args)
    return pl.pallas_call(
        body,
        out_shape=out,
        in_specs=specs,
        out_specs=[pl.BlockSpec(memory_space=pltpu.VMEM)] * len(out),
        scratch_shapes=list(scratch),
        compiler_params=pltpu.CompilerParams(vmem_limit_bytes=2 * size + (2 << 20)),
        cost_estimate=pl.CostEstimate(flops=flops, bytes_accessed=size, transcendentals=0),
    )(*args)


def shape(s, d=F32):
    return jax.ShapeDtypeStruct(s, d)


def cut(v):
    high = v.astype(BF16)
    return high, (v - high.astype(F32)).astype(BF16)


def dot(a, b, dims):
    return lax.dot_general(a, b, dims, preferred_element_type=F32)


def three(ah, al, bh, bl, dims):
    n = ah.shape[0]
    both = dot(jnp.concatenate([ah, al], axis=0), bh, dims)
    return both[:n] + both[n:] + dot(ah, bl, dims)


def split(v, rows=256):
    n, m = v.shape

    def body(v_ref, h_ref, l_ref):
        def step(i, _):
            s = pl.ds(pl.multiple_of(i * rows, rows), rows)
            h_ref[s], l_ref[s] = cut(v_ref[s])
            return 0

        lax.fori_loop(0, n // rows, step, 0)

    return call(body, [shape((n, m), BF16)] * 2, v)


def adjoint(blocks, order, part, count, k):
    low, length = blocks[0].shape
    nb = len(blocks)
    take = count // low
    width = k[0].shape[1]

    def body(*refs):
        b, kr, outs = refs[:nb], refs[nb : nb + 4], refs[nb + 4 :]
        me = lax.shift_right_logical(lax.axis_index("col"), 1)
        rows = []
        for i in range(part * take, (part + 1) * take):
            want = jnp.bitwise_xor(me, i)
            v = b[0][...]
            for j in range(1, nb):
                v = jnp.where(want == order[j], b[j][...], v)
            rows.append(v)
        xh, xl = cut(jnp.concatenate(rows, axis=0) if take > 1 else rows[0])
        ps = [three(xh, xl, kr[2 * j][...], kr[2 * j + 1][...], NN) for j in range(2)]
        odd = jnp.bitwise_and(lax.axis_index("row"), 1) == 1
        outs[0][...] = jnp.where(odd, ps[1], ps[0])
        outs[1][...] = jnp.where(odd, ps[0], ps[1])

    return call(
        body,
        [shape((count, width))] * 2,
        *blocks,
        *k,
        flops=12 * count * length * width,
    )


def spread(axis, blocks, order, out_rows):
    n = len(blocks)

    def body(*refs):
        h = blocks[0].shape[0]
        me = lax.axis_index(axis)
        for j in range(n):
            at = jnp.bitwise_xor(me, order[j]) * h
            refs[n][pl.ds(pl.multiple_of(at, 8), h)] = refs[j][...]

    return call(body, [shape((out_rows, blocks[0].shape[1]))], *blocks)[0]


def forward_all(a, k, t):
    n, width = a[0].shape
    rows, tops = k[0].shape[0], t[0].shape[0]
    total = rows + tops
    half = total // 2

    def body(*refs):
        ar, kr, tr, outs = refs[:2], refs[2:6], refs[6:10], refs[10:]
        odd = jnp.bitwise_and(lax.axis_index("row"), 1) == 1
        kept, got = ar[0][...], ar[1][...]
        parts = [cut(jnp.where(odd, got, kept)), cut(jnp.where(odd, kept, got))]
        step = 256
        for lo in range(0, total, step):
            src, at = (kr, lo) if lo < rows else (tr, lo - rows)
            size = min(step, (rows if lo < rows else total) - lo)
            s = slice(at, at + size)
            p = None
            for j in range(2):
                h, l = parts[j]
                q = three(h, l, src[2 * j][s], src[2 * j + 1][s], NT)
                p = q if p is None else p + q
            for o in range(2):
                b, e = max(lo, o * half), min(lo + size, (o + 1) * half)
                if b < e:
                    outs[o][:, b - o * half : e - o * half] = p[:, b - lo : e - lo]

    return call(
        body, [shape((n, half))] * 2, *a, *k, *t, flops=12 * n * total * width
    )


def picks(tags, anc, block, mode_local, sep_local, slots, cands):
    fanout = tags.shape[0]
    rows = fanout * block
    seps = fanout * sep_local
    modes = slots * fanout
    count = anc.shape[1]

    def body(tag_ref, anc_ref, p_ref, q_ref):
        lane = lax.broadcasted_iota(jnp.int32, (fanout, block), 1)
        hit = (tag_ref[...] == lax.axis_index("col").astype(F32)) & (lane < mode_local)
        ones = jnp.where(hit, 1.0, 0.0).astype(BF16)
        before = lax.broadcasted_iota(jnp.int32, (block, block), 0) < lax.broadcasted_iota(
            jnp.int32, (block, block), 1
        )
        rank = dot(ones, jnp.where(before, 1.0, 0.0).astype(BF16), NN).astype(jnp.int32)
        place = lax.broadcasted_iota(jnp.int32, (fanout, block), 0) * slots + rank
        place = jnp.where(hit, place, -1)
        sep = (lane >= mode_local) & (lane < mode_local + sep_local)
        home = modes + lax.broadcasted_iota(jnp.int32, (fanout, block), 0) * sep_local + lane - mode_local
        place = jnp.where(sep, home, place)
        row = lax.broadcasted_iota(jnp.int32, (modes + seps, block), 0)
        for f in range(fanout):
            p_ref[:, f * block : (f + 1) * block] = jnp.where(row == place[f : f + 1], 1.0, 0.0).astype(BF16)
        which = lax.broadcasted_iota(jnp.int32, (cands, count), 0)
        q_ref[...] = jnp.where(which == anc_ref[...], 1.0, 0.0).astype(BF16)

    return call(body, [shape((modes + seps, rows), BF16), shape((cands, count), BF16)], tags, anc)


def expand(nblocks, own, other, coup, p, q, leaf, cons, part, parts, block, prior):
    n, wide = own.shape
    rows = p.shape[1]
    modes = leaf.shape[1]
    seps = p.shape[0] - modes
    count = cons.shape[1]
    inter = leaf.shape[0]
    sep_local = block
    nv = 2 * n
    tile = 256
    low = n * parts // nblocks

    def body(own_ref, other_ref, ch, cl, p_ref, q_ref, l_ref, c_ref, *rest):
        (sep_ref, out_ref, f_ref, dh, dl) = rest[len(prior) :]

        @pl.when(pl.program_id(0) == 0)
        def _():
            parity = jnp.bitwise_and(lax.axis_index("col"), 1)
            for i in range(n // low):
                s = slice(i * low, (i + 1) * low)
                a = pl.multiple_of(2 * i * low + parity * low, 8)
                b = pl.multiple_of(2 * i * low + (1 - parity) * low, 8)
                f_ref[pl.ds(a, low)] = own_ref[s]
                f_ref[pl.ds(b, low)] = other_ref[s]
            fh, fl = cut(f_ref[...])
            both = jnp.concatenate([fh, fl], axis=0)
            got = dot(both[:, :rows], p_ref[...], NT)
            th, tl = fh[:, rows:], fl[:, rows:]
            raw = got[:nv, modes:] + got[nv:, modes:]
            sep = raw + three(th, tl, ch[...], cl[...], NT)
            sh, sl = cut(sep)
            cand = jnp.concatenate(
                [jnp.concatenate([th, sh], axis=1), jnp.concatenate([tl, sl], axis=1)], axis=0
            )
            found = dot(cand, q_ref[...], NN)
            dh[:, :modes] = got[:, :modes].astype(BF16)
            dh[:, modes:] = found.astype(BF16)
            dl[...] = sep.T
            mine = pl.multiple_of(lax.axis_index("col") * sep_local, 8)
            sep_ref[...] = dl[pl.ds(mine, sep_local)]

        lh, ll = cut(l_ref[...])
        kh, kl = cut(c_ref[...])
        wh = jnp.concatenate([lh, kh], axis=1)
        wl = jnp.concatenate([ll, kl], axis=1)
        d = dh[...]
        y = dot(wh, d, NT)
        out_ref[...] = y[:, :nv] + y[:, nv:] + dot(wl, d[:nv], NT)

    full = lambda a: pl.BlockSpec(a.shape, lambda i: (0,) * a.ndim)
    args = [own, other, *coup, p, q]
    return pl.pallas_call(
        body,
        grid=(inter // tile,),
        out_shape=[shape((sep_local, nv * parts)), shape((inter, nv * parts))],
        in_specs=[full(a) for a in args]
        + [
            pl.BlockSpec((tile, modes), lambda i: (i, 0)),
            pl.BlockSpec((tile, count), lambda i: (i, 0)),
        ]
        + [pl.BlockSpec(memory_space=pl.ANY)] * len(prior),
        out_specs=[
            pl.BlockSpec((sep_local, nv), lambda i: (0, part)),
            pl.BlockSpec((tile, nv), lambda i: (i, part)),
        ],
        scratch_shapes=[
            pltpu.VMEM((nv, wide), F32),
            pltpu.VMEM((2 * nv, modes + count), BF16),
            pltpu.VMEM((seps, nv), F32),
        ],
        input_output_aliases={8 + i: i for i in range(len(prior))},
        compiler_params=pltpu.CompilerParams(
            vmem_limit_bytes=4 * sum(a.size * a.dtype.itemsize for a in args) + (8 << 20)
        ),
        cost_estimate=pl.CostEstimate(
            flops=12 * inter * (modes + count) * nv,
            bytes_accessed=4 * inter * (modes + count + nv),
            transcendentals=0,
        ),
    )(*args, leaf, cons, *prior)


def spans(masks):
    found = [0]
    for m in masks:
        found = found + [o ^ m for o in found]
    return found


def on_device(operator, vectors, owner_map, coupling, ancestors, leaf_modes, constraint_modes):
    planes = lax.axis_size("row")
    fanout = lax.axis_size("col")
    mode_local = owner_map.shape[0]
    sep_local, top_count = coupling.shape[1:]
    leaf, cons = leaf_modes[0, 0], constraint_modes[0, 0]
    slots = leaf.shape[1] // fanout
    row_count, width = operator.shape
    block = row_count // fanout
    top_local = block - mode_local - sep_local
    row_masks = [1 << b for b in range(planes.bit_length() - 1)]
    col_masks = [1 << b for b in range(1, fanout.bit_length() - 1)]

    partner = swap(operator, "col", 1)
    xt = vectors.T
    col_order = spans(col_masks)
    blocks = [xt] + [swap(xt, "col", m) for m in col_order[1:]]
    tops = operator.reshape(fanout, block, width)[:, block - top_local :].reshape(-1, width)
    row_order = spans(row_masks)
    tops = [tops] + [swap(tops, "row", m) for m in row_order[1:]]
    k = split(operator)
    k = k + split(partner)

    parts = 2
    half_nv = xt.shape[0] * len(blocks)
    count = half_nv // parts
    order = [o // 2 for o in col_order]
    adj = []
    for h in range(parts):
        adj.append(list(adjoint(blocks, order, h, count, k)))
    tops = spread("row", list(tops), row_order, top_count)
    tops_partner = swap(tops, "col", 1)
    t = split(tops) + split(tops_partner)

    tag_rows = -(-mode_local // top_count)
    owner_map, coupling, _ = lax.optimization_barrier((owner_map, coupling, adj[1][0]))
    tags = owner_map[:, 0].astype(F32)
    tags = jnp.pad(tags, (0, tag_rows * top_count - mode_local), constant_values=-1.0).reshape(tag_rows, top_count)
    small = jnp.concatenate([coupling[0], jnp.pad(tags, ((0, -tag_rows % 8), (0, 0)))], axis=0)
    stack = small[None]
    for m in [1] + col_masks:
        stack = jnp.concatenate([stack, swap(stack, "col", m)], axis=0)
    small_order = spans([1] + col_masks)
    gathered = spread("col", list(stack), small_order, fanout * small.shape[0]).reshape(fanout, -1, top_count)
    coup = split(gathered[:, :sep_local].reshape(fanout * sep_local, top_count))
    tags = gathered[:, sep_local : sep_local + tag_rows].reshape(fanout, -1)[:, :block]
    p, q = picks(
        tags, ancestors[0], block, mode_local, sep_local, slots, top_count + fanout * sep_local
    )

    prior = ()
    for h in range(parts):
        a = list(adj[h])
        kept = a[0] + swap(a[1], "row", row_masks[0])
        for m in row_masks[1:]:
            kept = kept + swap(kept, "row", m)
        got = swap(kept, "row", row_masks[0])
        f = list(forward_all([kept, got], k, t))
        n = len(col_masks)
        for step in range(n):
            moved = [swap(v, "col", col_masks[(i + step) % n]) for i, v in enumerate(f)]
            f = [u + v for u, v in zip(f, moved)]
        own = jnp.concatenate(f, axis=1)
        other = swap(own, "col", 1)
        prior = expand(
            len(blocks), own, other, coup, p, q, leaf, cons, h, parts, sep_local, prior
        )
    return (prior[0][None], prior[1][None, None])


def solution(mesh):
    in_specs = (
        P("row", "col"),
        P("row", "col"),
        P(("row", "col"), None),
        P("row", "col", None),
        P("row", "col", None),
        P("row", "col", None, None),
        P("row", "col", None, None),
    )
    out_specs = (P("row", "col", None), P("row", "col", None, None))

    return jax.shard_map(on_device, mesh=mesh, in_specs=in_specs, out_specs=out_specs, check_vma=False)
```

```python
import jax
import jax.numpy as jnp
from jax import lax
from jax.experimental import pallas as pl
from jax.experimental.pallas import tpu as pltpu
from jax.sharding import PartitionSpec as P


F32, BF16 = jnp.float32, jnp.bfloat16
NN = (((1,), (0,)), ((), ()))
NT = (((1,), (1,)), ((), ()))


def swap(v, axis, mask):
    n = lax.axis_size(axis)
    return lax.ppermute(v, axis, [(i, i ^ mask) for i in range(n)])


def call(body, out, *args, scratch=(), flops=0):
    size = sum(a.size * a.dtype.itemsize for a in args) + sum(
        o.size * o.dtype.itemsize for o in out
    )
    specs = [pl.BlockSpec(memory_space=pltpu.VMEM)] * len(args)
    return pl.pallas_call(
        body,
        out_shape=out,
        in_specs=specs,
        out_specs=[pl.BlockSpec(memory_space=pltpu.VMEM)] * len(out),
        scratch_shapes=list(scratch),
        compiler_params=pltpu.CompilerParams(vmem_limit_bytes=2 * size + (2 << 20)),
        cost_estimate=pl.CostEstimate(flops=flops, bytes_accessed=size, transcendentals=0),
    )(*args)


def shape(s, d=F32):
    return jax.ShapeDtypeStruct(s, d)


def cut(v):
    high = v.astype(BF16)
    return high, (v - high.astype(F32)).astype(BF16)


def dot(a, b, dims):
    return lax.dot_general(a, b, dims, preferred_element_type=F32)


def three(ah, al, bh, bl, dims):
    n = ah.shape[0]
    both = dot(jnp.concatenate([ah, al], axis=0), bh, dims)
    return both[:n] + both[n:] + dot(ah, bl, dims)


def split(v, rows=256):
    n, m = v.shape

    def body(v_ref, h_ref, l_ref):
        def step(i, _):
            s = pl.ds(pl.multiple_of(i * rows, rows), rows)
            h_ref[s], l_ref[s] = cut(v_ref[s])
            return 0

        lax.fori_loop(0, n // rows, step, 0)

    return call(body, [shape((n, m), BF16)] * 2, v)


def adjoint(blocks, order, part, count, k):
    low, length = blocks[0].shape
    nb = len(blocks)
    take = count // low
    width = k[0].shape[1]

    def body(*refs):
        b, kr, outs = refs[:nb], refs[nb : nb + 4], refs[nb + 4 :]
        me = lax.shift_right_logical(lax.axis_index("col"), 1)
        rows = []
        for i in range(part * take, (part + 1) * take):
            want = jnp.bitwise_xor(me, i)
            v = b[0][...]
            for j in range(1, nb):
                v = jnp.where(want == order[j], b[j][...], v)
            rows.append(v)
        xh, xl = cut(jnp.concatenate(rows, axis=0) if take > 1 else rows[0])
        ps = [three(xh, xl, kr[2 * j][...], kr[2 * j + 1][...], NN) for j in range(2)]
        odd = jnp.bitwise_and(lax.axis_index("row"), 1) == 1
        outs[0][...] = jnp.where(odd, ps[1], ps[0])
        outs[1][...] = jnp.where(odd, ps[0], ps[1])

    return call(
        body,
        [shape((count, width))] * 2,
        *blocks,
        *k,
        flops=12 * count * length * width,
    )


def spread(axis, blocks, order, out_rows):
    n = len(blocks)

    def body(*refs):
        h = blocks[0].shape[0]
        me = lax.axis_index(axis)
        for j in range(n):
            at = jnp.bitwise_xor(me, order[j]) * h
            refs[n][pl.ds(pl.multiple_of(at, 8), h)] = refs[j][...]

    return call(body, [shape((out_rows, blocks[0].shape[1]))], *blocks)[0]


def forward_all(a, k, t):
    n, width = a[0].shape
    rows, tops = k[0].shape[0], t[0].shape[0]
    total = rows + tops
    half = total // 2

    def body(*refs):
        ar, kr, tr, outs = refs[:2], refs[2:6], refs[6:10], refs[10:]
        odd = jnp.bitwise_and(lax.axis_index("row"), 1) == 1
        kept, got = ar[0][...], ar[1][...]
        parts = [cut(jnp.where(odd, got, kept)), cut(jnp.where(odd, kept, got))]
        step = 256
        for lo in range(0, total, step):
            src, at = (kr, lo) if lo < rows else (tr, lo - rows)
            size = min(step, (rows if lo < rows else total) - lo)
            s = slice(at, at + size)
            p = None
            for j in range(2):
                h, l = parts[j]
                q = three(h, l, src[2 * j][s], src[2 * j + 1][s], NT)
                p = q if p is None else p + q
            for o in range(2):
                b, e = max(lo, o * half), min(lo + size, (o + 1) * half)
                if b < e:
                    outs[o][:, b - o * half : e - o * half] = p[:, b - lo : e - lo]

    return call(
        body, [shape((n, half))] * 2, *a, *k, *t, flops=12 * n * total * width
    )


def picks(tags, anc, block, mode_local, sep_local, slots, cands):
    fanout = tags.shape[0]
    rows = fanout * block
    seps = fanout * sep_local
    modes = slots * fanout
    count = anc.shape[1]

    def body(tag_ref, anc_ref, p_ref, q_ref):
        lane = lax.broadcasted_iota(jnp.int32, (fanout, block), 1)
        hit = (tag_ref[...] == lax.axis_index("col").astype(F32)) & (lane < mode_local)
        ones = jnp.where(hit, 1.0, 0.0).astype(BF16)
        before = lax.broadcasted_iota(jnp.int32, (block, block), 0) < lax.broadcasted_iota(
            jnp.int32, (block, block), 1
        )
        rank = dot(ones, jnp.where(before, 1.0, 0.0).astype(BF16), NN).astype(jnp.int32)
        place = lax.broadcasted_iota(jnp.int32, (fanout, block), 0) * slots + rank
        place = jnp.where(hit, place, -1)
        sep = (lane >= mode_local) & (lane < mode_local + sep_local)
        home = modes + lax.broadcasted_iota(jnp.int32, (fanout, block), 0) * sep_local + lane - mode_local
        place = jnp.where(sep, home, place)
        row = lax.broadcasted_iota(jnp.int32, (modes + seps, block), 0)
        for f in range(fanout):
            p_ref[:, f * block : (f + 1) * block] = jnp.where(row == place[f : f + 1], 1.0, 0.0).astype(BF16)
        which = lax.broadcasted_iota(jnp.int32, (count, cands), 1)
        wanted = jnp.broadcast_to(anc_ref[...], (8, count)).astype(F32).T[:, :1].astype(jnp.int32)
        q_ref[...] = jnp.where(which == wanted, 1.0, 0.0).astype(BF16)

    return call(body, [shape((modes + seps, rows), BF16), shape((count, cands), BF16)], tags, anc)


def expand(nblocks, own, other, coup, p, q, leaf, cons, part, parts, sep_local, prior):
    n, wide = own.shape
    rows = p.shape[1]
    inter, modes = leaf.shape
    seps = p.shape[0] - modes
    count = cons.shape[1]
    nv = 2 * n
    tile = 256
    low = n * parts // nblocks

    def body(own_ref, other_ref, ch, cl, p_ref, q_ref, l_ref, c_ref, *rest):
        sep_out, out, f_ref, d_ref, s_ref, y_ref, e_ref, sems = rest[len(prior) :]
        lanes = pl.ds(part * nv, nv)
        parity = jnp.bitwise_and(lax.axis_index("col"), 1)
        for i in range(n // low):
            s = slice(i * low, (i + 1) * low)
            a = pl.multiple_of(2 * i * low + parity * low, 8)
            b = pl.multiple_of(2 * i * low + (1 - parity) * low, 8)
            f_ref[pl.ds(a, low)] = own_ref[s]
            f_ref[pl.ds(b, low)] = other_ref[s]
        both = jnp.concatenate(cut(f_ref[:, :rows]), axis=0)
        got = dot(p_ref[...], both, NT)
        d_ref[:modes] = got[:modes].astype(BF16)
        raw = got[modes:, :nv] + got[modes:, nv:]
        th, tl = cut(f_ref[:, rows:].T)
        sep = raw + three(ch[...], cl[...], th, tl, NN)
        s_ref[...] = sep
        tops = jnp.concatenate([th, tl], axis=1)
        cand = jnp.concatenate([tops, jnp.concatenate(cut(sep), axis=1)], axis=0)
        d_ref[modes:] = dot(q_ref[...], cand, NN).astype(BF16)
        mine = pl.multiple_of(lax.axis_index("col") * sep_local, 8)
        e_ref[...] = s_ref[pl.ds(mine, sep_local)]

        def put(i):
            t = pl.ds(i * tile, tile)
            return pltpu.make_async_copy(y_ref.at[t], out.at[t, lanes], sems.at[i])

        sep_copy = pltpu.make_async_copy(e_ref, sep_out.at[:, lanes], sems.at[tiles])
        for i in range(tiles):
            t = slice(i * tile, (i + 1) * tile)
            lh, ll = cut(l_ref[t])
            kh, kl = cut(c_ref[t])
            y = dot(lh, d_ref[:modes], NN) + dot(kh, d_ref[modes:], NN)
            z = dot(ll, d_ref[:modes, :nv], NN) + dot(kl, d_ref[modes:, :nv], NN)
            y_ref[t] = y[:, :nv] + y[:, nv:] + z
            (sep_copy if i == 0 else put(i - 1)).start()
        put(tiles - 1).start()
        sep_copy.wait()
        for i in range(tiles):
            put(i).wait()

    args = [own, other, *coup, p, q, leaf, cons]
    tiles = inter // tile
    return pl.pallas_call(
        body,
        out_shape=[shape((sep_local, nv * parts)), shape((inter, nv * parts))],
        in_specs=[pl.BlockSpec(memory_space=pltpu.VMEM)] * len(args)
        + [pl.BlockSpec(memory_space=pl.ANY)] * len(prior),
        out_specs=[pl.BlockSpec(memory_space=pl.ANY)] * 2,
        scratch_shapes=[
            pltpu.VMEM((nv, wide), F32),
            pltpu.VMEM((modes + count, 2 * nv), BF16),
            pltpu.VMEM((seps, nv), F32),
            pltpu.VMEM((inter, nv), F32),
            pltpu.VMEM((sep_local, nv), F32),
            pltpu.SemaphoreType.DMA((tiles + 1,)),
        ],
        input_output_aliases={8 + i: i for i in range(len(prior))},
        compiler_params=pltpu.CompilerParams(
            vmem_limit_bytes=sum(a.size * a.dtype.itemsize for a in args) + (8 << 20)
        ),
        cost_estimate=pl.CostEstimate(
            flops=12 * inter * (modes + count) * nv,
            bytes_accessed=4 * inter * (modes + count + nv),
            transcendentals=0,
        ),
    )(*args, *prior)


def spans(masks):
    found = [0]
    for m in masks:
        found = found + [o ^ m for o in found]
    return found


def on_device(operator, vectors, owner_map, coupling, ancestors, leaf_modes, constraint_modes):
    planes = lax.axis_size("row")
    fanout = lax.axis_size("col")
    mode_local = owner_map.shape[0]
    sep_local, top_count = coupling.shape[1:]
    leaf, cons = leaf_modes[0, 0], constraint_modes[0, 0]
    slots = leaf.shape[1] // fanout
    row_count, width = operator.shape
    block = row_count // fanout
    top_local = block - mode_local - sep_local
    row_masks = [1 << b for b in range(planes.bit_length() - 1)]
    col_masks = [1 << b for b in range(1, fanout.bit_length() - 1)]

    partner = swap(operator, "col", 1)
    xt = vectors.T
    col_order = spans(col_masks)
    blocks = [xt] + [swap(xt, "col", m) for m in col_order[1:]]
    tops = operator.reshape(fanout, block, width)[:, block - top_local :].reshape(-1, width)
    row_order = spans(row_masks)
    tops = [tops] + [swap(tops, "row", m) for m in row_order[1:]]
    k = split(operator)
    k = k + split(partner)

    parts = 2
    half_nv = xt.shape[0] * len(blocks)
    count = half_nv // parts
    order = [o // 2 for o in col_order]
    adj = []
    for h in range(parts):
        adj.append(list(adjoint(blocks, order, h, count, k)))
    tops = spread("row", list(tops), row_order, top_count)
    tops_partner = swap(tops, "col", 1)
    t = split(tops) + split(tops_partner)

    tag_rows = -(-mode_local // top_count)
    owner_map, coupling, _ = lax.optimization_barrier((owner_map, coupling, adj[1][0]))
    tags = owner_map[:, 0].astype(F32)
    tags = jnp.pad(tags, (0, tag_rows * top_count - mode_local), constant_values=-1.0).reshape(tag_rows, top_count)
    small = jnp.concatenate([coupling[0], jnp.pad(tags, ((0, -tag_rows % 8), (0, 0)))], axis=0)
    stack = small[None]
    for m in [1] + col_masks:
        stack = jnp.concatenate([stack, swap(stack, "col", m)], axis=0)
    small_order = spans([1] + col_masks)
    gathered = spread("col", list(stack), small_order, fanout * small.shape[0]).reshape(fanout, -1, top_count)
    coup = split(gathered[:, :sep_local].reshape(fanout * sep_local, top_count))
    tags = gathered[:, sep_local : sep_local + tag_rows].reshape(fanout, -1)[:, :block]
    p, q = picks(
        tags, ancestors[0], block, mode_local, sep_local, slots, top_count + fanout * sep_local
    )

    prior = ()
    for h in range(parts):
        a = list(adj[h])
        kept = a[0] + swap(a[1], "row", row_masks[0])
        for m in row_masks[1:]:
            kept = kept + swap(kept, "row", m)
        got = swap(kept, "row", row_masks[0])
        f = list(forward_all([kept, got], k, t))
        n = len(col_masks)
        for step in range(n):
            moved = [swap(v, "col", col_masks[(i + step) % n]) for i, v in enumerate(f)]
            f = [u + v for u, v in zip(f, moved)]
        own = jnp.concatenate(f, axis=1)
        other = swap(own, "col", 1)
        prior = expand(
            len(blocks), own, other, coup, p, q, leaf, cons, h, parts, sep_local, prior
        )
    return (prior[0][None], prior[1][None, None])


def solution(mesh):
    in_specs = (
        P("row", "col"),
        P("row", "col"),
        P(("row", "col"), None),
        P("row", "col", None),
        P("row", "col", None),
        P("row", "col", None, None),
        P("row", "col", None, None),
    )
    out_specs = (P("row", "col", None), P("row", "col", None, None))

    return jax.shard_map(on_device, mesh=mesh, in_specs=in_specs, out_specs=out_specs, check_vma=False)
```

```python
import jax
import jax.numpy as jnp
from jax import lax
from jax.experimental import pallas as pl
from jax.experimental.pallas import tpu as pltpu
from jax.sharding import PartitionSpec as P


F32, BF16 = jnp.float32, jnp.bfloat16
NN = (((1,), (0,)), ((), ()))
NT = (((1,), (1,)), ((), ()))


def swap(v, axis, mask):
    n = lax.axis_size(axis)
    return lax.ppermute(v, axis, [(i, i ^ mask) for i in range(n)])


def call(body, out, *args, scratch=(), flops=0):
    size = sum(a.size * a.dtype.itemsize for a in args) + sum(
        o.size * o.dtype.itemsize for o in out
    )
    specs = [pl.BlockSpec(memory_space=pltpu.VMEM)] * len(args)
    return pl.pallas_call(
        body,
        out_shape=out,
        in_specs=specs,
        out_specs=[pl.BlockSpec(memory_space=pltpu.VMEM)] * len(out),
        scratch_shapes=list(scratch),
        compiler_params=pltpu.CompilerParams(vmem_limit_bytes=2 * size + (2 << 20)),
        cost_estimate=pl.CostEstimate(flops=flops, bytes_accessed=size, transcendentals=0),
    )(*args)


def shape(s, d=F32):
    return jax.ShapeDtypeStruct(s, d)


def cut(v):
    high = v.astype(BF16)
    return high, (v - high.astype(F32)).astype(BF16)


def dot(a, b, dims):
    return lax.dot_general(a, b, dims, preferred_element_type=F32)


def three(ah, al, bh, bl, dims):
    n = ah.shape[0]
    both = dot(jnp.concatenate([ah, al], axis=0), bh, dims)
    return both[:n] + both[n:] + dot(ah, bl, dims)


def split(v, rows=256):
    n, m = v.shape

    def body(v_ref, h_ref, l_ref):
        def step(i, _):
            s = pl.ds(pl.multiple_of(i * rows, rows), rows)
            h_ref[s], l_ref[s] = cut(v_ref[s])
            return 0

        lax.fori_loop(0, n // rows, step, 0)

    return call(body, [shape((n, m), BF16)] * 2, v)


def split_with_tops(v, fanout, tops, rows=256):
    n, m = v.shape
    block = n // fanout

    def body(v_ref, h_ref, l_ref, t_ref):
        for f in range(fanout):
            t_ref[f * tops : (f + 1) * tops] = v_ref[(f + 1) * block - tops : (f + 1) * block]

        def step(i, _):
            s = pl.ds(pl.multiple_of(i * rows, rows), rows)
            h_ref[s], l_ref[s] = cut(v_ref[s])
            return 0

        lax.fori_loop(0, n // rows, step, 0)

    return call(body, [shape((n, m), BF16)] * 2 + [shape((fanout * tops, m))], v)


def adjoint(blocks, order, part, count, k):
    low, length = blocks[0].shape
    nb = len(blocks)
    take = count // low
    width = k[0].shape[1]

    def body(*refs):
        b, kr, outs = refs[:nb], refs[nb : nb + 4], refs[nb + 4 :]
        me = lax.shift_right_logical(lax.axis_index("col"), 1)
        rows = []
        for i in range(part * take, (part + 1) * take):
            want = jnp.bitwise_xor(me, i)
            v = b[0][...]
            for j in range(1, nb):
                v = jnp.where(want == order[j], b[j][...], v)
            rows.append(v)
        xh, xl = cut(jnp.concatenate(rows, axis=0) if take > 1 else rows[0])
        ps = [three(xh, xl, kr[2 * j][...], kr[2 * j + 1][...], NN) for j in range(2)]
        odd = jnp.bitwise_and(lax.axis_index("row"), 1) == 1
        outs[0][...] = jnp.where(odd, ps[1], ps[0])
        outs[1][...] = jnp.where(odd, ps[0], ps[1])

    return call(
        body,
        [shape((count, width))] * 2,
        *blocks,
        *k,
        flops=12 * count * length * width,
    )


def spread(axis, blocks, order, out_rows):
    n = len(blocks)

    def body(*refs):
        h = blocks[0].shape[0]
        me = lax.axis_index(axis)
        for j in range(n):
            at = jnp.bitwise_xor(me, order[j]) * h
            refs[n][pl.ds(pl.multiple_of(at, 8), h)] = refs[j][...]

    return call(body, [shape((out_rows, blocks[0].shape[1]))], *blocks)[0]


def forward_all(a, k, t):
    n, width = a[0].shape
    rows, tops = k[0].shape[0], t[0].shape[0]
    total = rows + tops
    half = total // 2

    def body(*refs):
        ar, kr, tr, outs = refs[:2], refs[2:6], refs[6:10], refs[10:]
        odd = jnp.bitwise_and(lax.axis_index("row"), 1) == 1
        kept, got = ar[0][...], ar[1][...]
        parts = [cut(jnp.where(odd, got, kept)), cut(jnp.where(odd, kept, got))]
        step = 256
        for lo in range(0, total, step):
            src, at = (kr, lo) if lo < rows else (tr, lo - rows)
            size = min(step, (rows if lo < rows else total) - lo)
            s = slice(at, at + size)
            p = None
            for j in range(2):
                h, l = parts[j]
                q = three(h, l, src[2 * j][s], src[2 * j + 1][s], NT)
                p = q if p is None else p + q
            for o in range(2):
                b, e = max(lo, o * half), min(lo + size, (o + 1) * half)
                if b < e:
                    outs[o][:, b - o * half : e - o * half] = p[:, b - lo : e - lo]

    return call(
        body, [shape((n, half))] * 2, *a, *k, *t, flops=12 * n * total * width
    )


def picks(tags, anc, block, mode_local, sep_local, slots, cands):
    fanout = tags.shape[0]
    rows = fanout * block
    seps = fanout * sep_local
    modes = slots * fanout
    count = anc.shape[1]

    def body(tag_ref, anc_ref, p_ref, q_ref):
        lane = lax.broadcasted_iota(jnp.int32, (fanout, block), 1)
        hit = (tag_ref[...] == lax.axis_index("col").astype(F32)) & (lane < mode_local)
        ones = jnp.where(hit, 1.0, 0.0).astype(BF16)
        before = lax.broadcasted_iota(jnp.int32, (block, block), 0) < lax.broadcasted_iota(
            jnp.int32, (block, block), 1
        )
        rank = dot(ones, jnp.where(before, 1.0, 0.0).astype(BF16), NN).astype(jnp.int32)
        place = lax.broadcasted_iota(jnp.int32, (fanout, block), 0) * slots + rank
        place = jnp.where(hit, place, -1)
        sep = (lane >= mode_local) & (lane < mode_local + sep_local)
        home = modes + lax.broadcasted_iota(jnp.int32, (fanout, block), 0) * sep_local + lane - mode_local
        place = jnp.where(sep, home, place)
        row = lax.broadcasted_iota(jnp.int32, (modes + seps, block), 0)
        for f in range(fanout):
            p_ref[:, f * block : (f + 1) * block] = jnp.where(row == place[f : f + 1], 1.0, 0.0).astype(BF16)
        which = lax.broadcasted_iota(jnp.int32, (count, cands), 1)
        wanted = jnp.broadcast_to(anc_ref[...], (8, count)).astype(F32).T[:, :1].astype(jnp.int32)
        q_ref[...] = jnp.where(which == wanted, 1.0, 0.0).astype(BF16)

    return call(body, [shape((modes + seps, rows), BF16), shape((count, cands), BF16)], tags, anc)


def expand(nblocks, own, other, coup, p, q, leaf, cons, part, parts, sep_local, prior):
    n, wide = own.shape
    rows = p.shape[1]
    inter, modes = leaf.shape
    seps = p.shape[0] - modes
    count = cons.shape[1]
    nv = 2 * n
    tile = 256
    low = n * parts // nblocks

    def body(own_ref, other_ref, ch, cl, p_ref, q_ref, l_ref, c_ref, *rest):
        sep_out, out, f_ref, d_ref, s_ref, y_ref, e_ref, sems = rest[len(prior) :]
        lanes = pl.ds(part * nv, nv)
        parity = jnp.bitwise_and(lax.axis_index("col"), 1)
        for i in range(n // low):
            s = slice(i * low, (i + 1) * low)
            a = pl.multiple_of(2 * i * low + parity * low, 8)
            b = pl.multiple_of(2 * i * low + (1 - parity) * low, 8)
            f_ref[pl.ds(a, low)] = own_ref[s]
            f_ref[pl.ds(b, low)] = other_ref[s]
        both = jnp.concatenate(cut(f_ref[:, :rows]), axis=0)
        got = dot(p_ref[...], both, NT)
        d_ref[:modes] = got[:modes].astype(BF16)
        raw = got[modes:, :nv] + got[modes:, nv:]
        th, tl = cut(f_ref[:, rows:].T)
        sep = raw + three(ch[...], cl[...], th, tl, NN)
        s_ref[...] = sep
        tops = jnp.concatenate([th, tl], axis=1)
        cand = jnp.concatenate([tops, jnp.concatenate(cut(sep), axis=1)], axis=0)
        d_ref[modes:] = dot(q_ref[...], cand, NN).astype(BF16)
        mine = pl.multiple_of(lax.axis_index("col") * sep_local, 8)
        e_ref[...] = s_ref[pl.ds(mine, sep_local)]

        def put(i):
            t = pl.ds(i * tile, tile)
            return pltpu.make_async_copy(y_ref.at[t], out.at[t, lanes], sems.at[i])

        sep_copy = pltpu.make_async_copy(e_ref, sep_out.at[:, lanes], sems.at[tiles])
        for i in range(tiles):
            t = slice(i * tile, (i + 1) * tile)
            lh, ll = cut(l_ref[t])
            kh, kl = cut(c_ref[t])
            y = dot(lh, d_ref[:modes], NN) + dot(kh, d_ref[modes:], NN)
            z = dot(ll, d_ref[:modes, :nv], NN) + dot(kl, d_ref[modes:, :nv], NN)
            y_ref[t] = y[:, :nv] + y[:, nv:] + z
            (sep_copy if i == 0 else put(i - 1)).start()
        put(tiles - 1).start()
        sep_copy.wait()
        for i in range(tiles):
            put(i).wait()

    args = [own, other, *coup, p, q, leaf, cons]
    tiles = inter // tile
    return pl.pallas_call(
        body,
        out_shape=[shape((sep_local, nv * parts)), shape((inter, nv * parts))],
        in_specs=[pl.BlockSpec(memory_space=pltpu.VMEM)] * len(args)
        + [pl.BlockSpec(memory_space=pl.ANY)] * len(prior),
        out_specs=[pl.BlockSpec(memory_space=pl.ANY)] * 2,
        scratch_shapes=[
            pltpu.VMEM((nv, wide), F32),
            pltpu.VMEM((modes + count, 2 * nv), BF16),
            pltpu.VMEM((seps, nv), F32),
            pltpu.VMEM((inter, nv), F32),
            pltpu.VMEM((sep_local, nv), F32),
            pltpu.SemaphoreType.DMA((tiles + 1,)),
        ],
        input_output_aliases={8 + i: i for i in range(len(prior))},
        compiler_params=pltpu.CompilerParams(
            vmem_limit_bytes=sum(a.size * a.dtype.itemsize for a in args) + (8 << 20)
        ),
        cost_estimate=pl.CostEstimate(
            flops=12 * inter * (modes + count) * nv,
            bytes_accessed=4 * inter * (modes + count + nv),
            transcendentals=0,
        ),
    )(*args, *prior)


def spans(masks):
    found = [0]
    for m in masks:
        found = found + [o ^ m for o in found]
    return found


def on_device(operator, vectors, owner_map, coupling, ancestors, leaf_modes, constraint_modes):
    planes = lax.axis_size("row")
    fanout = lax.axis_size("col")
    mode_local = owner_map.shape[0]
    sep_local, top_count = coupling.shape[1:]
    leaf, cons = leaf_modes[0, 0], constraint_modes[0, 0]
    slots = leaf.shape[1] // fanout
    row_count, _ = operator.shape
    block = row_count // fanout
    top_local = block - mode_local - sep_local
    row_masks = [1 << b for b in range(planes.bit_length() - 1)]
    col_masks = [1 << b for b in range(1, fanout.bit_length() - 1)]

    partner = swap(operator, "col", 1)
    xt = vectors.T
    col_order = spans(col_masks)
    blocks = [xt] + [swap(xt, "col", m) for m in col_order[1:]]
    *k, tops = split_with_tops(operator, fanout, top_local)
    k = [*k, *split(partner)]
    row_order = spans(row_masks)
    tops = [tops] + [swap(tops, "row", m) for m in row_order[1:]]
    tops = spread("row", tops, row_order, top_count)
    tops_partner = swap(tops, "col", 1)
    t = split(tops) + split(tops_partner)

    parts = 2
    half_nv = xt.shape[0] * len(blocks)
    count = half_nv // parts
    order = [o // 2 for o in col_order]
    adj = []
    for h in range(parts):
        adj.append(list(adjoint(blocks, order, h, count, k)))
    tag_rows = -(-mode_local // top_count)
    owner_map, coupling, _ = lax.optimization_barrier((owner_map, coupling, adj[1][0]))
    tags = owner_map[:, 0].astype(F32)
    tags = jnp.pad(tags, (0, tag_rows * top_count - mode_local), constant_values=-1.0).reshape(tag_rows, top_count)
    small = jnp.concatenate([coupling[0], jnp.pad(tags, ((0, -tag_rows % 8), (0, 0)))], axis=0)
    stack = small[None]
    for m in [1] + col_masks:
        stack = jnp.concatenate([stack, swap(stack, "col", m)], axis=0)
    small_order = spans([1] + col_masks)
    gathered = spread("col", list(stack), small_order, fanout * small.shape[0]).reshape(fanout, -1, top_count)
    coup = split(gathered[:, :sep_local].reshape(fanout * sep_local, top_count))
    tags = gathered[:, sep_local : sep_local + tag_rows].reshape(fanout, -1)[:, :block]
    p, q = picks(
        tags, ancestors[0], block, mode_local, sep_local, slots, top_count + fanout * sep_local
    )

    prior = ()
    for h in range(parts):
        a = list(adj[h])
        kept = a[0] + swap(a[1], "row", row_masks[0])
        for m in row_masks[1:]:
            kept = kept + swap(kept, "row", m)
        got = swap(kept, "row", row_masks[0])
        f = list(forward_all([kept, got], k, t))
        n = len(col_masks)
        for step in range(n):
            moved = [swap(v, "col", col_masks[(i + step) % n]) for i, v in enumerate(f)]
            f = [u + v for u, v in zip(f, moved)]
        own = jnp.concatenate(f, axis=1)
        other = swap(own, "col", 1)
        prior = expand(
            len(blocks), own, other, coup, p, q, leaf, cons, h, parts, sep_local, prior
        )
    return (prior[0][None], prior[1][None, None])


def solution(mesh):
    in_specs = (
        P("row", "col"),
        P("row", "col"),
        P(("row", "col"), None),
        P("row", "col", None),
        P("row", "col", None),
        P("row", "col", None, None),
        P("row", "col", None, None),
    )
    out_specs = (P("row", "col", None), P("row", "col", None, None))

    return jax.shard_map(on_device, mesh=mesh, in_specs=in_specs, out_specs=out_specs, check_vma=False)
```

```python
import jax
import jax.numpy as jnp
from jax import lax
from jax.experimental import pallas as pl
from jax.experimental.pallas import tpu as pltpu
from jax.sharding import PartitionSpec as P


F32, BF16 = jnp.float32, jnp.bfloat16
NN = (((1,), (0,)), ((), ()))
NT = (((1,), (1,)), ((), ()))


def swap(v, axis, mask):
    n = lax.axis_size(axis)
    return lax.ppermute(v, axis, [(i, i ^ mask) for i in range(n)])


def call(body, out, *args, scratch=(), flops=0):
    size = sum(a.size * a.dtype.itemsize for a in args) + sum(
        o.size * o.dtype.itemsize for o in out
    )
    specs = [pl.BlockSpec(memory_space=pltpu.VMEM)] * len(args)
    return pl.pallas_call(
        body,
        out_shape=out,
        in_specs=specs,
        out_specs=[pl.BlockSpec(memory_space=pltpu.VMEM)] * len(out),
        scratch_shapes=list(scratch),
        compiler_params=pltpu.CompilerParams(vmem_limit_bytes=2 * size + (2 << 20)),
        cost_estimate=pl.CostEstimate(flops=flops, bytes_accessed=size, transcendentals=0),
    )(*args)


def shape(s, d=F32):
    return jax.ShapeDtypeStruct(s, d)


def cut(v):
    high = v.astype(BF16)
    return high, (v - high.astype(F32)).astype(BF16)


def dot(a, b, dims):
    return lax.dot_general(a, b, dims, preferred_element_type=F32)


def three(ah, al, bh, bl, dims):
    n = ah.shape[0]
    both = dot(jnp.concatenate([ah, al], axis=0), bh, dims)
    return both[:n] + both[n:] + dot(ah, bl, dims)


def split(v, rows=256):
    n, m = v.shape

    def body(v_ref, h_ref, l_ref):
        def step(i, _):
            s = pl.ds(pl.multiple_of(i * rows, rows), rows)
            h_ref[s], l_ref[s] = cut(v_ref[s])
            return 0

        lax.fori_loop(0, n // rows, step, 0)

    return call(body, [shape((n, m), BF16)] * 2, v)


def split_with_tops(v, fanout, tops, rows=256):
    n, m = v.shape
    block = n // fanout

    def body(v_ref, h_ref, l_ref, t_ref):
        for f in range(fanout):
            t_ref[f * tops : (f + 1) * tops] = v_ref[(f + 1) * block - tops : (f + 1) * block]

        def step(i, _):
            s = pl.ds(pl.multiple_of(i * rows, rows), rows)
            h_ref[s], l_ref[s] = cut(v_ref[s])
            return 0

        lax.fori_loop(0, n // rows, step, 0)

    return call(body, [shape((n, m), BF16)] * 2 + [shape((fanout * tops, m))], v)


def adjoint(blocks, order, part, count, k):
    low, length = blocks[0].shape
    nb = len(blocks)
    take = count // low
    width = k[0].shape[1]

    def body(*refs):
        b, kr, outs = refs[:nb], refs[nb : nb + 4], refs[nb + 4 :]
        me = lax.shift_right_logical(lax.axis_index("col"), 1)
        rows = []
        for i in range(part * take, (part + 1) * take):
            want = jnp.bitwise_xor(me, i)
            v = b[0][...]
            for j in range(1, nb):
                v = jnp.where(want == order[j], b[j][...], v)
            rows.append(v)
        xh, xl = cut(jnp.concatenate(rows, axis=0) if take > 1 else rows[0])
        ps = [three(xh, xl, kr[2 * j][...], kr[2 * j + 1][...], NN) for j in range(2)]
        odd = jnp.bitwise_and(lax.axis_index("row"), 1) == 1
        outs[0][...] = jnp.where(odd, ps[1], ps[0])
        outs[1][...] = jnp.where(odd, ps[0], ps[1])

    return call(
        body,
        [shape((count, width))] * 2,
        *blocks,
        *k,
        flops=12 * count * length * width,
    )


def spread(axis, blocks, order, out_rows):
    n = len(blocks)

    def body(*refs):
        h = blocks[0].shape[0]
        me = lax.axis_index(axis)
        for j in range(n):
            at = jnp.bitwise_xor(me, order[j]) * h
            refs[n][pl.ds(pl.multiple_of(at, 8), h)] = refs[j][...]

    return call(body, [shape((out_rows, blocks[0].shape[1]))], *blocks)[0]


def forward_all(a, k, t):
    n, width = a[0].shape
    rows, tops = k[0].shape[0], t[0].shape[0]
    total = rows + tops
    half = total // 2

    def body(*refs):
        ar, kr, tr, outs = refs[:2], refs[2:6], refs[6:10], refs[10:]
        odd = jnp.bitwise_and(lax.axis_index("row"), 1) == 1
        kept, got = ar[0][...], ar[1][...]
        parts = [cut(jnp.where(odd, got, kept)), cut(jnp.where(odd, kept, got))]
        step = 256
        for lo in range(0, total, step):
            src, at = (kr, lo) if lo < rows else (tr, lo - rows)
            size = min(step, (rows if lo < rows else total) - lo)
            s = slice(at, at + size)
            y = z = None
            for j in range(2):
                h, l = parts[j]
                u = dot(src[2 * j][s], jnp.concatenate([h, l], axis=0), NT)
                v = dot(src[2 * j + 1][s], h, NT)
                y, z = (u, v) if y is None else (y + u, z + v)
            y = y.T
            p = y[:n] + y[n:] + z.T
            for o in range(2):
                b, e = max(lo, o * half), min(lo + size, (o + 1) * half)
                if b < e:
                    outs[o][:, b - o * half : e - o * half] = p[:, b - lo : e - lo]

    return call(
        body, [shape((n, half))] * 2, *a, *k, *t, flops=12 * n * total * width
    )


def picks(tags, anc, block, mode_local, sep_local, slots, cands):
    fanout = tags.shape[0]
    group = slots + sep_local
    count = anc.shape[1]

    def body(tag_ref, anc_ref, p_ref, q_ref):
        lane = lax.broadcasted_iota(jnp.int32, (fanout, block), 1)
        hit = (tag_ref[...] == lax.axis_index("col").astype(F32)) & (lane < mode_local)
        ones = jnp.where(hit, 1.0, 0.0).astype(BF16)
        before = lax.broadcasted_iota(jnp.int32, (block, block), 0) < lax.broadcasted_iota(
            jnp.int32, (block, block), 1
        )
        rank = dot(ones, jnp.where(before, 1.0, 0.0).astype(BF16), NN).astype(jnp.int32)
        sep = (lane >= mode_local) & (lane < mode_local + sep_local)
        place = jnp.where(sep, slots + lane - mode_local, jnp.where(hit, rank, -1))
        row = lax.broadcasted_iota(jnp.int32, (group, block), 0)
        for f in range(fanout):
            p_ref[f * group : (f + 1) * group] = jnp.where(row == place[f : f + 1], 1.0, 0.0).astype(BF16)
        which = lax.broadcasted_iota(jnp.int32, (count, cands), 1)
        wanted = jnp.broadcast_to(anc_ref[...], (8, count)).astype(F32).T[:, :1].astype(jnp.int32)
        q_ref[...] = jnp.where(which == wanted, 1.0, 0.0).astype(BF16)

    return call(body, [shape((fanout * group, block), BF16), shape((count, cands), BF16)], tags, anc)


def expand(nblocks, own, other, coup, p, q, leaf, cons, part, parts, sep_local, prior):
    n, wide = own.shape
    group, block = sep_local + leaf.shape[1] * p.shape[1] // (wide - coup[0].shape[1]), p.shape[1]
    fanout = p.shape[0] // group
    rows, slots = fanout * block, group - sep_local
    inter, modes = leaf.shape
    seps = fanout * sep_local
    count = cons.shape[1]
    nv = 2 * n
    tile = 256
    low = n * parts // nblocks

    def body(own_ref, other_ref, ch, cl, p_ref, q_ref, l_ref, c_ref, *rest):
        sep_out, out, f_ref, d_ref, s_ref, y_ref, e_ref, sems = rest[len(prior) :]
        lanes = pl.ds(part * nv, nv)
        parity = jnp.bitwise_and(lax.axis_index("col"), 1)
        for i in range(n // low):
            s = slice(i * low, (i + 1) * low)
            a = pl.multiple_of(2 * i * low + parity * low, 8)
            b = pl.multiple_of(2 * i * low + (1 - parity) * low, 8)
            f_ref[pl.ds(a, low)] = own_ref[s]
            f_ref[pl.ds(b, low)] = other_ref[s]
        both = jnp.concatenate(cut(f_ref[:, :rows]), axis=0)
        raw = []
        for f in range(fanout):
            got = dot(p_ref[f * group : (f + 1) * group], both[:, f * block : (f + 1) * block], NT)
            d_ref[f * slots : (f + 1) * slots] = got[:slots].astype(BF16)
            raw.append(got[slots:, :nv] + got[slots:, nv:])
        th, tl = cut(f_ref[:, rows:].T)
        sep = jnp.concatenate(raw, axis=0) + three(ch[...], cl[...], th, tl, NN)
        s_ref[...] = sep
        tops = jnp.concatenate([th, tl], axis=1)
        cand = jnp.concatenate([tops, jnp.concatenate(cut(sep), axis=1)], axis=0)
        d_ref[modes:] = dot(q_ref[...], cand, NN).astype(BF16)
        mine = pl.multiple_of(lax.axis_index("col") * sep_local, 8)
        e_ref[...] = s_ref[pl.ds(mine, sep_local)]

        def put(i):
            t = pl.ds(i * tile, tile)
            return pltpu.make_async_copy(y_ref.at[t], out.at[t, lanes], sems.at[i])

        sep_copy = pltpu.make_async_copy(e_ref, sep_out.at[:, lanes], sems.at[tiles])
        for i in range(tiles):
            t = slice(i * tile, (i + 1) * tile)
            lh, ll = cut(l_ref[t])
            kh, kl = cut(c_ref[t])
            y = dot(lh, d_ref[:modes], NN) + dot(kh, d_ref[modes:], NN)
            z = dot(ll, d_ref[:modes, :nv], NN) + dot(kl, d_ref[modes:, :nv], NN)
            y_ref[t] = y[:, :nv] + y[:, nv:] + z
            (sep_copy if i == 0 else put(i - 1)).start()
        put(tiles - 1).start()
        sep_copy.wait()
        for i in range(tiles):
            put(i).wait()

    args = [own, other, *coup, p, q, leaf, cons]
    tiles = inter // tile
    return pl.pallas_call(
        body,
        out_shape=[shape((sep_local, nv * parts)), shape((inter, nv * parts))],
        in_specs=[pl.BlockSpec(memory_space=pltpu.VMEM)] * len(args)
        + [pl.BlockSpec(memory_space=pl.ANY)] * len(prior),
        out_specs=[pl.BlockSpec(memory_space=pl.ANY)] * 2,
        scratch_shapes=[
            pltpu.VMEM((nv, wide), F32),
            pltpu.VMEM((modes + count, 2 * nv), BF16),
            pltpu.VMEM((seps, nv), F32),
            pltpu.VMEM((inter, nv), F32),
            pltpu.VMEM((sep_local, nv), F32),
            pltpu.SemaphoreType.DMA((tiles + 1,)),
        ],
        input_output_aliases={8 + i: i for i in range(len(prior))},
        compiler_params=pltpu.CompilerParams(
            vmem_limit_bytes=sum(a.size * a.dtype.itemsize for a in args) + (8 << 20)
        ),
        cost_estimate=pl.CostEstimate(
            flops=12 * inter * (modes + count) * nv,
            bytes_accessed=4 * inter * (modes + count + nv),
            transcendentals=0,
        ),
    )(*args, *prior)


def spans(masks):
    found = [0]
    for m in masks:
        found = found + [o ^ m for o in found]
    return found


def on_device(operator, vectors, owner_map, coupling, ancestors, leaf_modes, constraint_modes):
    planes = lax.axis_size("row")
    fanout = lax.axis_size("col")
    mode_local = owner_map.shape[0]
    sep_local, top_count = coupling.shape[1:]
    leaf, cons = leaf_modes[0, 0], constraint_modes[0, 0]
    slots = leaf.shape[1] // fanout
    row_count, _ = operator.shape
    block = row_count // fanout
    top_local = block - mode_local - sep_local
    row_masks = [1 << b for b in range(planes.bit_length() - 1)]
    col_masks = [1 << b for b in range(1, fanout.bit_length() - 1)]

    partner = swap(operator, "col", 1)
    xt = vectors.T
    col_order = spans(col_masks)
    blocks = [xt] + [swap(xt, "col", m) for m in col_order[1:]]
    *k, tops = split_with_tops(operator, fanout, top_local)
    k = [*k, *split(partner)]
    row_order = spans(row_masks)
    tops = [tops] + [swap(tops, "row", m) for m in row_order[1:]]
    tops = spread("row", tops, row_order, top_count)
    tops_partner = swap(tops, "col", 1)
    t = split(tops) + split(tops_partner)

    parts = 2
    half_nv = xt.shape[0] * len(blocks)
    count = half_nv // parts
    order = [o // 2 for o in col_order]
    adj = []
    for h in range(parts):
        adj.append(list(adjoint(blocks, order, h, count, k)))
    tag_rows = -(-mode_local // top_count)
    owner_map, coupling, _ = lax.optimization_barrier((owner_map, coupling, adj[1][0]))
    tags = owner_map[:, 0].astype(F32)
    tags = jnp.pad(tags, (0, tag_rows * top_count - mode_local), constant_values=-1.0).reshape(tag_rows, top_count)
    small = jnp.concatenate([coupling[0], jnp.pad(tags, ((0, -tag_rows % 8), (0, 0)))], axis=0)
    stack = small[None]
    for m in [1] + col_masks:
        stack = jnp.concatenate([stack, swap(stack, "col", m)], axis=0)
    small_order = spans([1] + col_masks)
    gathered = spread("col", list(stack), small_order, fanout * small.shape[0]).reshape(fanout, -1, top_count)
    coup = split(gathered[:, :sep_local].reshape(fanout * sep_local, top_count))
    tags = gathered[:, sep_local : sep_local + tag_rows].reshape(fanout, -1)[:, :block]
    p, q = picks(
        tags, ancestors[0], block, mode_local, sep_local, slots, top_count + fanout * sep_local
    )

    prior = ()
    for h in range(parts):
        a = list(adj[h])
        kept = a[0] + swap(a[1], "row", row_masks[0])
        for m in row_masks[1:]:
            kept = kept + swap(kept, "row", m)
        got = swap(kept, "row", row_masks[0])
        f = list(forward_all([kept, got], k, t))
        n = len(col_masks)
        for step in range(n):
            moved = [swap(v, "col", col_masks[(i + step) % n]) for i, v in enumerate(f)]
            f = [u + v for u, v in zip(f, moved)]
        own = jnp.concatenate(f, axis=1)
        other = swap(own, "col", 1)
        prior = expand(
            len(blocks), own, other, coup, p, q, leaf, cons, h, parts, sep_local, prior
        )
    return (prior[0][None], prior[1][None, None])


def solution(mesh):
    in_specs = (
        P("row", "col"),
        P("row", "col"),
        P(("row", "col"), None),
        P("row", "col", None),
        P("row", "col", None),
        P("row", "col", None, None),
        P("row", "col", None, None),
    )
    out_specs = (P("row", "col", None), P("row", "col", None, None))

    return jax.shard_map(on_device, mesh=mesh, in_specs=in_specs, out_specs=out_specs, check_vma=False)
```

```python
import jax
import jax.numpy as jnp
from jax import lax
from jax.experimental import pallas as pl
from jax.experimental.pallas import tpu as pltpu
from jax.sharding import PartitionSpec as P


F32, BF16 = jnp.float32, jnp.bfloat16
NN = (((1,), (0,)), ((), ()))
NT = (((1,), (1,)), ((), ()))


def swap(v, axis, mask):
    n = lax.axis_size(axis)
    return lax.ppermute(v, axis, [(i, i ^ mask) for i in range(n)])


def call(body, out, *args, scratch=(), flops=0):
    size = sum(a.size * a.dtype.itemsize for a in args) + sum(
        o.size * o.dtype.itemsize for o in out
    )
    specs = [pl.BlockSpec(memory_space=pltpu.VMEM)] * len(args)
    return pl.pallas_call(
        body,
        out_shape=out,
        in_specs=specs,
        out_specs=[pl.BlockSpec(memory_space=pltpu.VMEM)] * len(out),
        scratch_shapes=list(scratch),
        compiler_params=pltpu.CompilerParams(vmem_limit_bytes=2 * size + (2 << 20)),
        cost_estimate=pl.CostEstimate(flops=flops, bytes_accessed=size, transcendentals=0),
    )(*args)


def shape(s, d=F32):
    return jax.ShapeDtypeStruct(s, d)


def cut(v):
    high = v.astype(BF16)
    return high, (v - high.astype(F32)).astype(BF16)


def dot(a, b, dims):
    return lax.dot_general(a, b, dims, preferred_element_type=F32)


def three(ah, al, bh, bl, dims):
    n = ah.shape[0]
    both = dot(jnp.concatenate([ah, al], axis=0), bh, dims)
    return both[:n] + both[n:] + dot(ah, bl, dims)


def split(v, rows=256):
    n, m = v.shape

    def body(v_ref, h_ref, l_ref):
        def step(i, _):
            s = pl.ds(pl.multiple_of(i * rows, rows), rows)
            h_ref[s], l_ref[s] = cut(v_ref[s])
            return 0

        lax.fori_loop(0, n // rows, step, 0)

    return call(body, [shape((n, m), BF16)] * 2, v)


def split_with_tops(v, fanout, tops, rows=256):
    n, m = v.shape
    block = n // fanout

    def body(v_ref, h_ref, l_ref, t_ref):
        for f in range(fanout):
            t_ref[f * tops : (f + 1) * tops] = v_ref[(f + 1) * block - tops : (f + 1) * block]

        def step(i, _):
            s = pl.ds(pl.multiple_of(i * rows, rows), rows)
            h_ref[s], l_ref[s] = cut(v_ref[s])
            return 0

        lax.fori_loop(0, n // rows, step, 0)

    return call(body, [shape((n, m), BF16)] * 2 + [shape((fanout * tops, m))], v)


def adjoint(blocks, order, part, count, k):
    low, length = blocks[0].shape
    nb = len(blocks)
    take = count // low
    width = k[0].shape[1]

    def body(*refs):
        b, kr, outs = refs[:nb], refs[nb : nb + 4], refs[nb + 4 :]
        me = lax.shift_right_logical(lax.axis_index("col"), 1)
        rows = []
        for i in range(part * take, (part + 1) * take):
            want = jnp.bitwise_xor(me, i)
            v = b[0][...]
            for j in range(1, nb):
                v = jnp.where(want == order[j], b[j][...], v)
            rows.append(v)
        xh, xl = cut(jnp.concatenate(rows, axis=0) if take > 1 else rows[0])
        ps = [three(xh, xl, kr[2 * j][...], kr[2 * j + 1][...], NN) for j in range(2)]
        odd = jnp.bitwise_and(lax.axis_index("row"), 1) == 1
        outs[0][...] = jnp.where(odd, ps[1], ps[0])
        outs[1][...] = jnp.where(odd, ps[0], ps[1])

    return call(
        body,
        [shape((count, width))] * 2,
        *blocks,
        *k,
        flops=12 * count * length * width,
    )


def spread(axis, blocks, order, out_rows):
    n = len(blocks)

    def body(*refs):
        h = blocks[0].shape[0]
        me = lax.axis_index(axis)
        for j in range(n):
            at = jnp.bitwise_xor(me, order[j]) * h
            refs[n][pl.ds(pl.multiple_of(at, 8), h)] = refs[j][...]

    return call(body, [shape((out_rows, blocks[0].shape[1]))], *blocks)[0]


def forward_all(a, k, t):
    n, width = a[0].shape
    rows, tops = k[0].shape[0], t[0].shape[0]
    total = rows + tops
    half = total // 2

    def body(*refs):
        ar, kr, tr, outs = refs[:2], refs[2:6], refs[6:10], refs[10:]
        odd = jnp.bitwise_and(lax.axis_index("row"), 1) == 1
        kept, got = ar[0][...], ar[1][...]
        parts = [cut(jnp.where(odd, got, kept)), cut(jnp.where(odd, kept, got))]
        step = 256
        for lo in range(0, total, step):
            src, at = (kr, lo) if lo < rows else (tr, lo - rows)
            size = min(step, (rows if lo < rows else total) - lo)
            s = slice(at, at + size)
            y = z = None
            for j in range(2):
                h, l = parts[j]
                u = dot(src[2 * j][s], jnp.concatenate([h, l], axis=0), NT)
                v = dot(src[2 * j + 1][s], h, NT)
                y, z = (u, v) if y is None else (y + u, z + v)
            y = y.T
            p = y[:n] + y[n:] + z.T
            for o in range(2):
                b, e = max(lo, o * half), min(lo + size, (o + 1) * half)
                if b < e:
                    outs[o][:, b - o * half : e - o * half] = p[:, b - lo : e - lo]

    return call(
        body, [shape((n, half))] * 2, *a, *k, *t, flops=12 * n * total * width
    )


def picks(tags, anc, block, mode_local, sep_local, slots, cands):
    fanout = tags.shape[0]
    group = slots + sep_local
    count = anc.shape[1]

    def body(tag_ref, anc_ref, p_ref, q_ref):
        lane = lax.broadcasted_iota(jnp.int32, (fanout, block), 1)
        hit = (tag_ref[...] == lax.axis_index("col").astype(F32)) & (lane < mode_local)
        ones = jnp.where(hit, 1.0, 0.0).astype(BF16)
        before = lax.broadcasted_iota(jnp.int32, (block, block), 0) < lax.broadcasted_iota(
            jnp.int32, (block, block), 1
        )
        rank = dot(ones, jnp.where(before, 1.0, 0.0).astype(BF16), NN).astype(jnp.int32)
        sep = (lane >= mode_local) & (lane < mode_local + sep_local)
        place = jnp.where(sep, slots + lane - mode_local, jnp.where(hit, rank, -1))
        row = lax.broadcasted_iota(jnp.int32, (group, block), 0)
        for f in range(fanout):
            p_ref[f * group : (f + 1) * group] = jnp.where(row == place[f : f + 1], 1.0, 0.0).astype(BF16)
        which = lax.broadcasted_iota(jnp.int32, (count, cands), 1)
        wanted = jnp.broadcast_to(anc_ref[...], (8, count)).astype(F32).T[:, :1].astype(jnp.int32)
        q_ref[...] = jnp.where(which == wanted, 1.0, 0.0).astype(BF16)

    return call(body, [shape((fanout * group, block), BF16), shape((count, cands), BF16)], tags, anc)


def expand(nblocks, own, other, coup, p, q, leaf, cons, part, parts, sep_local, prior):
    n, wide = own.shape
    group, block = sep_local + leaf.shape[1] * p.shape[1] // (wide - coup[0].shape[1]), p.shape[1]
    fanout = p.shape[0] // group
    rows, slots = fanout * block, group - sep_local
    inter, modes = leaf.shape
    seps = fanout * sep_local
    count = cons.shape[1]
    nv = 2 * n
    tile = 128
    low = n * parts // nblocks

    def body(own_ref, other_ref, ch, cl, p_ref, q_ref, l_ref, c_ref, *rest):
        sep_out, out, f_ref, d_ref, s_ref, y_ref, e_ref, sems = rest[len(prior) :]
        lanes = pl.ds(part * nv, nv)
        parity = jnp.bitwise_and(lax.axis_index("col"), 1)
        for i in range(n // low):
            s = slice(i * low, (i + 1) * low)
            a = pl.multiple_of(2 * i * low + parity * low, 8)
            b = pl.multiple_of(2 * i * low + (1 - parity) * low, 8)
            f_ref[pl.ds(a, low)] = own_ref[s]
            f_ref[pl.ds(b, low)] = other_ref[s]
        both = jnp.concatenate(cut(f_ref[:, :rows]), axis=0)
        raw = []
        for f in range(fanout):
            got = dot(p_ref[f * group : (f + 1) * group], both[:, f * block : (f + 1) * block], NT)
            d_ref[f * slots : (f + 1) * slots] = got[:slots].astype(BF16)
            raw.append(got[slots:, :nv] + got[slots:, nv:])
        th, tl = cut(f_ref[:, rows:].T)
        sep = jnp.concatenate(raw, axis=0) + three(ch[...], cl[...], th, tl, NN)
        s_ref[...] = sep
        tops = jnp.concatenate([th, tl], axis=1)
        cand = jnp.concatenate([tops, jnp.concatenate(cut(sep), axis=1)], axis=0)
        d_ref[modes:] = dot(q_ref[...], cand, NN).astype(BF16)
        mine = pl.multiple_of(lax.axis_index("col") * sep_local, 8)
        e_ref[...] = s_ref[pl.ds(mine, sep_local)]

        def put(i):
            t = pl.ds(i * tile, tile)
            return pltpu.make_async_copy(y_ref.at[t], out.at[t, lanes], sems.at[i])

        sep_copy = pltpu.make_async_copy(e_ref, sep_out.at[:, lanes], sems.at[tiles])
        for i in range(tiles):
            t = slice(i * tile, (i + 1) * tile)
            lh, ll = cut(l_ref[t])
            kh, kl = cut(c_ref[t])
            y = dot(lh, d_ref[:modes], NN) + dot(kh, d_ref[modes:], NN)
            z = dot(ll, d_ref[:modes, :nv], NN) + dot(kl, d_ref[modes:, :nv], NN)
            y_ref[t] = y[:, :nv] + y[:, nv:] + z
            (sep_copy if i == 0 else put(i - 1)).start()
        put(tiles - 1).start()
        sep_copy.wait()
        for i in range(tiles):
            put(i).wait()

    args = [own, other, *coup, p, q, leaf, cons]
    tiles = inter // tile
    return pl.pallas_call(
        body,
        out_shape=[shape((sep_local, nv * parts)), shape((inter, nv * parts))],
        in_specs=[pl.BlockSpec(memory_space=pltpu.VMEM)] * len(args)
        + [pl.BlockSpec(memory_space=pl.ANY)] * len(prior),
        out_specs=[pl.BlockSpec(memory_space=pl.ANY)] * 2,
        scratch_shapes=[
            pltpu.VMEM((nv, wide), F32),
            pltpu.VMEM((modes + count, 2 * nv), BF16),
            pltpu.VMEM((seps, nv), F32),
            pltpu.VMEM((inter, nv), F32),
            pltpu.VMEM((sep_local, nv), F32),
            pltpu.SemaphoreType.DMA((tiles + 1,)),
        ],
        input_output_aliases={8 + i: i for i in range(len(prior))},
        compiler_params=pltpu.CompilerParams(vmem_limit_bytes=sum(a.size * a.dtype.itemsize for a in args) + (8 << 20)),
        cost_estimate=pl.CostEstimate(
            flops=12 * inter * (modes + count) * nv,
            bytes_accessed=4 * inter * (modes + count + nv),
            transcendentals=0,
        ),
    )(*args, *prior)


def spans(masks):
    found = [0]
    for m in masks:
        found = found + [o ^ m for o in found]
    return found


def on_device(operator, vectors, owner_map, coupling, ancestors, leaf_modes, constraint_modes):
    planes = lax.axis_size("row")
    fanout = lax.axis_size("col")
    mode_local = owner_map.shape[0]
    sep_local, top_count = coupling.shape[1:]
    leaf, cons = leaf_modes[0, 0], constraint_modes[0, 0]
    slots = leaf.shape[1] // fanout
    row_count, _ = operator.shape
    block = row_count // fanout
    top_local = block - mode_local - sep_local
    row_masks = [1 << b for b in range(planes.bit_length() - 1)]
    col_masks = [1 << b for b in range(1, fanout.bit_length() - 1)]

    partner = swap(operator, "col", 1)
    xt = vectors.T
    col_order = spans(col_masks)
    blocks = [xt] + [swap(xt, "col", m) for m in col_order[1:]]
    *k, tops = split_with_tops(operator, fanout, top_local)
    k = [*k, *split(partner)]
    row_order = spans(row_masks)
    tops = [tops] + [swap(tops, "row", m) for m in row_order[1:]]
    tops = spread("row", tops, row_order, top_count)
    tops_partner = swap(tops, "col", 1)
    t = split(tops) + split(tops_partner)

    parts = 2
    half_nv = xt.shape[0] * len(blocks)
    count = half_nv // parts
    order = [o // 2 for o in col_order]
    adj = []
    for h in range(parts):
        adj.append(list(adjoint(blocks, order, h, count, k)))
    tag_rows = -(-mode_local // top_count)
    owner_map, coupling, _ = lax.optimization_barrier((owner_map, coupling, adj[1][0]))
    tags = owner_map[:, 0].astype(F32)
    tags = jnp.pad(tags, (0, tag_rows * top_count - mode_local), constant_values=-1.0).reshape(tag_rows, top_count)
    small = jnp.concatenate([coupling[0], jnp.pad(tags, ((0, -tag_rows % 8), (0, 0)))], axis=0)
    stack = small[None]
    for m in [1] + col_masks:
        stack = jnp.concatenate([stack, swap(stack, "col", m)], axis=0)
    small_order = spans([1] + col_masks)
    gathered = spread("col", list(stack), small_order, fanout * small.shape[0]).reshape(fanout, -1, top_count)
    coup = split(gathered[:, :sep_local].reshape(fanout * sep_local, top_count))
    tags = gathered[:, sep_local : sep_local + tag_rows].reshape(fanout, -1)[:, :block]
    p, q = picks(
        tags, ancestors[0], block, mode_local, sep_local, slots, top_count + fanout * sep_local
    )

    prior = ()
    for h in range(parts):
        a = list(adj[h])
        kept = a[0] + swap(a[1], "row", row_masks[0])
        for m in row_masks[1:]:
            kept = kept + swap(kept, "row", m)
        got = swap(kept, "row", row_masks[0])
        f = list(forward_all([kept, got], k, t))
        n = len(col_masks)
        for step in range(n):
            moved = [swap(v, "col", col_masks[(i + step) % n]) for i, v in enumerate(f)]
            f = [u + v for u, v in zip(f, moved)]
        own = jnp.concatenate(f, axis=1)
        other = swap(own, "col", 1)
        prior = expand(
            len(blocks), own, other, coup, p, q, leaf, cons, h, parts, sep_local, prior
        )
    return (prior[0][None], prior[1][None, None])


def solution(mesh):
    in_specs = (
        P("row", "col"),
        P("row", "col"),
        P(("row", "col"), None),
        P("row", "col", None),
        P("row", "col", None),
        P("row", "col", None, None),
        P("row", "col", None, None),
    )
    out_specs = (P("row", "col", None), P("row", "col", None, None))

    return jax.shard_map(on_device, mesh=mesh, in_specs=in_specs, out_specs=out_specs, check_vma=False)
```
